32 devices in a mesh: replica: 8 (over z, core), group: 4 (over y, x).
Axes of the slice: x: 2, y: 2, z: 4, core: 2. Of those that a mesh axis runs over, the one named last changes fastest.
Arguments:
- tokens: bfloat16 [4, 8192, 768], P('group', 'replica'), may hold values from -6 to 6
- cotangent: bfloat16 [4, 8192, 768], P('group', 'replica'), may hold values from -6 to 6
- lengths: int32 [4, 16], P('group'), may hold values from 256 to 768, as said below
- dealing: int32 [4, 16], P('group'), may hold values from 0 to 15, as said below
- offsets: int32 [4, 8, 2], P('group'), may hold values from 0 to 768, as said below
- attn_gain: float32 [768], P('group'), may hold values from 0.1 to 1.9
- qkv_weight: float32 [768, 2304], P('group'), may hold values from -0.21875 to 0.21875
- out_weight: float32 [768, 768], P('group'), may hold values from -0.875 to 0.875
- mlp_gain: float32 [768], P('group'), may hold values from 0.1 to 1.9
- in_weight: float32 [768, 2304], P('group'), may hold values from -0.21875 to 0.21875
- down_weight: float32 [1152, 768], P('group'), may hold values from -0.1875 to 0.1875
Outputs:
- output: bfloat16 [4, 8192, 768], P('group', 'replica')
- input_grad: bfloat16 [4, 8192, 768], P('group', 'replica')
- attn_gain_grad: float32 [768], P('group')
- qkv_grad: float32 [768, 2304], P('group')
- out_grad: float32 [768, 768], P('group')
- mlp_gain_grad: float32 [768], P('group')
- in_grad: float32 [768, 2304], P('group')
- down_grad: float32 [1152, 768], P('group')
The draws below stay inside these ranges and needn't reach their ends.
Inputs may be any that keep to these rules, and one draw needn't show every extreme that they name: `lengths`: the 16 sequences of a column lie end to end over its 8192 tokens; the two sequences dealt to one replica index hold 1024 tokens together. `dealing`: for each column a permutation of its sequences: entry k is the given-order number of the sequence that is k-th in dealt order; replica index r takes dealt sequences 2 * r to 2 * r + 1. `offsets`: exclusive running sums of the lengths of each replica index's dealt sequences, in dealt order.
All inputs are finite; a program needn't handle non-finite values.
Results may differ from the reference program's by a relative error of at most 0.02.
Values may be sent and summed in bfloat16 or wider, within the bound.
No kernel may reach another device: no remote copies, remote signals or barrier semaphores. Data moves between devices by JAX's collectives and lax.ppermute only.
A program may use at most 256 MiB of HBM per device.

```python
import math
import jax
import jax.numpy as jnp
from jax import lax

D = 768
HEADS = 12
HEAD_DIM = 64
FF = 1152
TOK_DEV = 1024
MINLEN = 256
TOK_COL = 8192
SEQ_COL = 16
N_REPLICA = 8
N_GROUP = 4


def dealt_plan(key):
    base = jax.random.fold_in(key, 11)
    first_key, forced_key, order_key = jax.random.split(base, 3)
    first_len = jax.random.randint(first_key, (N_GROUP, N_REPLICA), MINLEN, TOK_DEV - MINLEN + 1)
    forced = jax.random.randint(forced_key, (N_GROUP, 1), 0, N_REPLICA)
    columns = jnp.arange(N_REPLICA)[None, :]
    first_len = jnp.where(columns == forced, MINLEN, first_len)
    first_len = jnp.where(columns == (forced + 1) % N_REPLICA, TOK_DEV - MINLEN, first_len)
    dealt_len = jnp.stack([first_len, TOK_DEV - first_len], axis=-1).reshape(N_GROUP, SEQ_COL)
    orders = jax.vmap(lambda sub_key: jax.random.permutation(sub_key, SEQ_COL))(jax.random.split(order_key, N_GROUP))
    inverse = jnp.argsort(orders, axis=-1)
    given_len = jnp.take_along_axis(dealt_len, inverse, axis=-1)
    starts = jnp.stack([jnp.zeros_like(first_len), first_len], axis=-1)
    return (given_len.astype(jnp.int32), orders.astype(jnp.int32), starts.astype(jnp.int32))


def draw_lengths(key, part):
    return dealt_plan(key)[0]


def draw_dealing(key, part):
    return dealt_plan(key)[1]


def draw_offsets(key, part):
    return dealt_plan(key)[2]


def shard_levels(rng, shape, cuts, least, top_value):
    gain, own = 1.0, jax.random.fold_in(rng, 6)
    for dim, shards_of in cuts:
        heights = jnp.exp(jax.random.uniform(jax.random.fold_in(own, dim), (shards_of,), jnp.float32, least / len(cuts), top_value / len(cuts)))
        gain = gain * jnp.repeat(heights, shape[dim] // shards_of).reshape([-1 if axis == dim else 1 for axis in range(len(shape))])
    return gain


def normal_values(rng, dims, scale, most, cuts=(), kind=jnp.bfloat16):
    values = scale * jax.random.normal(rng, dims, jnp.float32)
    if cuts:
        values = values * shard_levels(rng, dims, cuts, -0.22, 0.18)
    return jnp.clip(values, -most, most).astype(kind)


def setup_inputs(seed: int = 0) -> dict:
    arg_keys = jax.random.split(jax.random.key(seed), 12)
    return {
        "tokens": normal_values(arg_keys[0], (N_GROUP, TOK_COL, D), 1.0, 6.0, ((0, 4), (1, 8))),
        "cotangent": normal_values(arg_keys[1], (N_GROUP, TOK_COL, D), 1.0, 6.0, ((0, 4), (1, 8))),
        "lengths": draw_lengths(jax.random.fold_in(arg_keys[11], 71), 0),
        "dealing": draw_dealing(jax.random.fold_in(arg_keys[11], 71), 0),
        "offsets": draw_offsets(jax.random.fold_in(arg_keys[11], 71), 0),
        "attn_gain": jnp.clip(1.0 + 0.18 * jax.random.normal(arg_keys[5], (D,), jnp.float32), 0.1, 1.9),
        "qkv_weight": normal_values(arg_keys[6], (D, 3 * D), D ** -0.5, 0.21875, ((0, 4),), jnp.float32),
        "out_weight": normal_values(arg_keys[7], (D, D), (D // 16) ** -0.5, 0.875, ((0, 4),), jnp.float32),
        "mlp_gain": jnp.clip(1.0 + 0.18 * jax.random.normal(arg_keys[8], (D,), jnp.float32), 0.1, 1.9),
        "in_weight": normal_values(arg_keys[9], (D, 2 * FF), D ** -0.5, 0.21875, ((0, 4),), jnp.float32),
        "down_weight": normal_values(arg_keys[10], (FF, D), FF ** -0.5, 0.1875, ((0, 4),), jnp.float32),
    }


@jax.custom_vjp
def low(v):
    return lax.optimization_barrier(v.astype(jnp.bfloat16)).astype(jnp.float32)

@jax.custom_vjp
def low_back(v):
    return v

def low_keep(v):
    return (low(v), None)

def low_pass(kept, grad):
    return (grad,)

def back_keep(v):
    return (v, None)

def back_low(kept, grad):
    return (low(grad),)
low.defvjp(low_keep, low_pass)
low_back.defvjp(back_keep, back_low)
epsilon = 1e-05
big_negative = -1e+30
rope_base = 160000.0

def column_starts(lengths):
    return (jnp.cumsum(lengths) - lengths).astype(jnp.int32)

def dealt_map(lengths, dealing, offsets, replica_index, tok_rows):
    seq_count = lengths.shape[0]
    per_device = offsets.shape[1]
    starts = column_starts(lengths)
    slot_ids = jnp.arange(tok_rows, dtype=jnp.int32)
    own_starts = lax.dynamic_index_in_dim(offsets, replica_index, 0, keepdims=False)
    segment = lax.optimization_barrier(jnp.sum((slot_ids[:, None] >= own_starts[None, 1:]).astype(jnp.int32), axis=1)).astype(jnp.int32)
    choose = segment[:, None] == jnp.arange(per_device, dtype=jnp.int32)[None, :]
    begin_at = lax.optimization_barrier(jnp.sum(jnp.where(choose, own_starts[None, :], 0), axis=1)).astype(jnp.int32)
    positions = (slot_ids - begin_at).astype(jnp.int32)
    dealt = (replica_index * per_device + segment).astype(jnp.int32)
    seq_range = jnp.arange(seq_count, dtype=jnp.int32)
    dealt_hits = dealt[:, None] == seq_range[None, :]
    given = lax.optimization_barrier(jnp.sum(jnp.where(dealt_hits, dealing[None, :], 0), axis=1)).astype(jnp.int32)
    found_seq = given[:, None] == seq_range[None, :]
    first_at = lax.optimization_barrier(jnp.sum(jnp.where(found_seq, starts[None, :], 0), axis=1)).astype(jnp.int32)
    source = jnp.clip(first_at + positions, 0, tok_rows * offsets.shape[0] - 1).astype(jnp.int32)
    return (source, segment, positions)

def given_map(lengths, dealing, offsets, column_pos, tok_rows):
    seq_count = lengths.shape[0]
    per_device = offsets.shape[1]
    starts = column_starts(lengths)
    seq_range = jnp.arange(seq_count, dtype=jnp.int32)
    seq_id = lax.optimization_barrier(jnp.sum((column_pos[:, None] >= starts[None, 1:]).astype(jnp.int32), axis=1)).astype(jnp.int32)
    found_seq = seq_id[:, None] == seq_range[None, :]
    first_at = lax.optimization_barrier(jnp.sum(jnp.where(found_seq, starts[None, :], 0), axis=1)).astype(jnp.int32)
    positions = column_pos - first_at
    matches = dealing[None, :] == seq_id[:, None]
    dealt = lax.optimization_barrier(jnp.sum(jnp.where(matches, seq_range[None, :], 0), axis=1)).astype(jnp.int32)
    flat_starts = offsets.reshape(-1)
    dealt_hits = dealt[:, None] == seq_range[None, :]
    begin_at = lax.optimization_barrier(jnp.sum(jnp.where(dealt_hits, flat_starts[None, :], 0), axis=1)).astype(jnp.int32)
    target = dealt // per_device * tok_rows + begin_at + positions
    return jnp.clip(target, 0, tok_rows * offsets.shape[0] - 1).astype(jnp.int32)

def rotary(values, positions, head_count, head_dim):
    tok_rows = values.shape[0]
    half_dim = head_dim // 2
    frequency = jnp.exp(-(jnp.arange(half_dim, dtype=jnp.float32) * (2.0 / head_dim)) * math.log(rope_base))
    angles = positions.astype(jnp.float32)[:, None] * frequency[None, :]
    cosine = jnp.cos(angles)[:, None, :]
    sine_part = jnp.sin(angles)[:, None, :]
    shaped = values.reshape(tok_rows, head_count, head_dim)
    lower_half = shaped[..., :half_dim]
    upper_half = shaped[..., half_dim:]
    turned = jnp.concatenate([lower_half * cosine - upper_half * sine_part, upper_half * cosine + lower_half * sine_part], axis=-1)
    return turned.reshape(tok_rows, head_count * head_dim)

def layer_norm(values, gain_vec):
    row_mean = lax.optimization_barrier(jnp.mean(values, axis=-1, keepdims=True))
    centred = values - row_mean
    spread = lax.optimization_barrier(jnp.mean(centred * centred, axis=-1, keepdims=True))
    return centred * lax.rsqrt(spread + epsilon) * gain_vec

def matmul(left, right):
    return jnp.dot(left, right, precision=lax.Precision.HIGHEST)

def attend_block(queries, seg_query, key_heads, value_heads, seg_keys):
    score_scale = HEAD_DIM ** (-0.5)
    scores = jnp.einsum('qhd,khd->hqk', queries, key_heads, precision=lax.Precision.HIGHEST) * score_scale
    scores = low_back(scores)
    same_seq = seg_query[:, None] == seg_keys[None, :]
    masked = jnp.where(same_seq[None], scores, big_negative)
    row_top = lax.optimization_barrier(jnp.max(masked, axis=-1, keepdims=True))
    exponent = jnp.exp(masked - row_top)
    row_total = lax.optimization_barrier(jnp.sum(exponent, axis=-1, keepdims=True))
    weights_soft = low(exponent / row_total)
    attended = jnp.einsum('hqk,khd->qhd', weights_soft, value_heads, precision=lax.Precision.HIGHEST)
    return low(low_back(attended))

def layer(rows_in, segment, positions, weights):
    gain_one, w_qkv, w_out, gain_two, w_in, w_down = weights
    tok_rows, model_width = rows_in.shape
    normed = low(layer_norm(rows_in, gain_one))
    mixed_proj = low_back(matmul(normed, w_qkv))
    queries = low(rotary(mixed_proj[:, :model_width], positions, HEADS, HEAD_DIM)).reshape(tok_rows, HEADS, HEAD_DIM)
    key_heads = low(rotary(mixed_proj[:, model_width:2 * model_width], positions, HEADS, HEAD_DIM)).reshape(tok_rows, HEADS, HEAD_DIM)
    value_heads = low(mixed_proj[:, 2 * model_width:]).reshape(tok_rows, HEADS, HEAD_DIM)
    block_rows = min(512, tok_rows)
    block_count = tok_rows // block_rows
    query_blocks = queries.reshape(block_count, block_rows, HEADS, HEAD_DIM)
    seg_blocks = segment.reshape(block_count, block_rows)

    def one_block(pair_item):
        return attend_block(pair_item[0], pair_item[1], key_heads, value_heads, segment)
    attended = lax.map(jax.checkpoint(one_block), (query_blocks, seg_blocks)).reshape(tok_rows, model_width)
    branch = low_back(matmul(attended, w_out))
    middle = rows_in + branch
    normed_two = low(layer_norm(middle, gain_two))
    lifted = low_back(matmul(normed_two, w_in))
    hidden = low(jax.nn.gelu(lifted[:, :FF], approximate=False) * lifted[:, FF:])
    return middle + low_back(matmul(hidden, w_down))

def reference(tokens, cotangent, lengths, dealing, offsets, attn_gain, qkv_weight, out_weight, mlp_gain, in_weight, down_weight):
    replicas = jnp.arange(N_REPLICA, dtype=jnp.int32)

    def column_plan(col_lengths, col_dealing, col_offsets):
        source, segment, positions = jax.vmap(lambda replica_index: dealt_map(col_lengths, col_dealing, col_offsets, replica_index, TOK_DEV))(replicas)
        target = given_map(col_lengths, col_dealing, col_offsets, jnp.arange(TOK_COL, dtype=jnp.int32), TOK_DEV)
        return (source, segment, positions, target)
    source, segment, positions, target = jax.vmap(column_plan)(lengths, dealing, offsets)
    seg_flat = segment.reshape(N_GROUP * N_REPLICA, TOK_DEV)
    pos_flat = positions.reshape(N_GROUP * N_REPLICA, TOK_DEV)

    def forward(inputs, gain_one, w_qkv, w_out, gain_two, w_in, w_down):
        weights = (low(gain_one), low(w_qkv), low(w_out), low(gain_two), low(w_in), low(w_down))
        dealt = jax.vmap(lambda col_rows, col_source: col_rows[col_source])(inputs, source.reshape(N_GROUP, TOK_COL))
        dealt = dealt.reshape(N_GROUP * N_REPLICA, TOK_DEV, inputs.shape[2])

        def run_block(rows_in, seg_block, pos_block):
            return layer(rows_in, seg_block, pos_block, weights)
        checked = jax.checkpoint(run_block)

        def scan_step(carry, scan_item):
            return (carry, checked(scan_item[0], scan_item[1], scan_item[2]))
        _, results = lax.scan(scan_step, jnp.zeros((), jnp.float32), (dealt, seg_flat, pos_flat))
        results = results.reshape(N_GROUP, TOK_COL, inputs.shape[2])
        return jax.vmap(lambda col_rows, col_target: col_rows[col_target])(results, target)
    floats = (tokens.astype(jnp.float32), attn_gain, qkv_weight, out_weight, mlp_gain, in_weight, down_weight)
    result, pullback = jax.vjp(forward, *floats)
    grads = pullback(cotangent.astype(jnp.float32))
    return (result.astype(jnp.bfloat16), grads[0].astype(jnp.bfloat16), grads[1], grads[2], grads[3], grads[4], grads[5], grads[6])
```

```python
import functools
import math

import jax
import jax.numpy as jnp
from jax import lax
from jax.experimental import pallas as pl
from jax.experimental.pallas import tpu as pltpu
from jax.sharding import PartitionSpec as P

HEADS = 12
HEAD_DIM = 64
PAIR = 2 * HEAD_DIM
MAX_LENGTH = 768

BLOCK = 256
epsilon = 1e-05
big_negative = -1e30
rope_base = 160000.0

bf16 = jnp.bfloat16
f32 = jnp.float32


def dot_nn(a, b):
    return lax.dot_general(a, b, (((1,), (0,)), ((), ())), preferred_element_type=f32)


def dot_nt(a, b):
    return lax.dot_general(a, b, (((1,), (1,)), ((), ())), preferred_element_type=f32)


def dot_tn(a, b):
    return lax.dot_general(a, b, (((0,), (0,)), ((), ())), preferred_element_type=f32)


def normalized(values):
    centred = values - jnp.mean(values, axis=-1, keepdims=True)
    spread = jnp.mean(centred * centred, axis=-1, keepdims=True)
    scale = lax.rsqrt(spread + epsilon)
    return centred * scale, scale


def turn(values, cosine, sine):
    lane = lax.broadcasted_iota(jnp.int32, values.shape, 1) % HEAD_DIM
    half = HEAD_DIM // 2
    other = jnp.where(
        lane < half, pltpu.roll(values, PAIR - half, 1), pltpu.roll(values, half, 1)
    )
    return values * cosine + other * sine


def params(**kw):
    return pltpu.CompilerParams(vmem_limit_bytes=60 * 1024 * 1024, **kw)


def qkv_body(ahead, own, bounds, x_ref, g_ref, w_ref, cos_ref, sin_ref, n_ref, q_ref, k_ref, v_ref):
    step = pl.program_id(0)
    width = x_ref.shape[1]
    needed = (step >= bounds[0]) & (step < bounds[1])

    @pl.when(needed)
    def _():
        normed, _ = normalized(x_ref[...].astype(f32))
        n1 = (normed * g_ref[...]).astype(bf16)
        n_ref[...] = n1
        cosine = cos_ref[...]
        sine = sin_ref[...]
        keys = dot_nn(n1, w_ref[:, width : 2 * width])
        for at in range(0, width, PAIR):
            k_ref[:, at : at + PAIR] = turn(keys[:, at : at + PAIR], cosine, sine).astype(bf16)
        v_ref[...] = dot_nn(n1, w_ref[:, 2 * width :]).astype(bf16)

        @pl.when((step >= ahead) & (step < ahead + own))
        def _():
            queries = dot_nn(n1, w_ref[:, :width])
            for at in range(0, width, PAIR):
                turned = turn(queries[:, at : at + PAIR], cosine, sine).astype(bf16)
                q_ref[:, at : at + PAIR] = turned * bf16(HEAD_DIM**-0.5)

    @pl.when(jnp.logical_not(needed))
    def _():
        n_ref[...] = jnp.zeros_like(n_ref)
        k_ref[...] = jnp.zeros_like(k_ref)
        v_ref[...] = jnp.zeros_like(v_ref)


def project(bounds, rows, gain, w_qkv, cosine, sine, own_rows):
    total, width = rows.shape
    ahead = MAX_LENGTH // BLOCK
    own = own_rows // BLOCK
    row = lambda i, b: (i, 0)
    whole = lambda i, b: (0, 0)
    own_row = lambda i, b: (jnp.clip(i - ahead, 0, own - 1), 0)
    return pl.pallas_call(
        functools.partial(qkv_body, ahead, own),
        grid_spec=pltpu.PrefetchScalarGridSpec(
            num_scalar_prefetch=1,
            grid=(total // BLOCK,),
            in_specs=[
                pl.BlockSpec((BLOCK, width), row),
                pl.BlockSpec((1, width), whole),
                pl.BlockSpec(w_qkv.shape, whole, pipeline_mode=pl.Buffered(1)),
                pl.BlockSpec((BLOCK, PAIR), row),
                pl.BlockSpec((BLOCK, PAIR), row),
            ],
            out_specs=[
                pl.BlockSpec((BLOCK, width), row),
                pl.BlockSpec((BLOCK, width), own_row),
                pl.BlockSpec((BLOCK, width), row),
                pl.BlockSpec((BLOCK, width), row),
            ],
        ),
        out_shape=[
            jax.ShapeDtypeStruct((total, width), bf16),
            jax.ShapeDtypeStruct((own_rows, width), bf16),
            jax.ShapeDtypeStruct((total, width), bf16),
            jax.ShapeDtypeStruct((total, width), bf16),
        ],
        compiler_params=params(),
        name="project",
    )(bounds, rows, gain, w_qkv, cosine, sine)


def head_lanes(shape, head):
    lane = lax.broadcasted_iota(jnp.int32, shape, 1)
    return lane < HEAD_DIM if head == 0 else lane >= HEAD_DIM


def inside(span_ref, key_row, shape):
    key = lax.broadcasted_iota(jnp.int32, shape, 0) + key_row
    return (key >= span_ref[0:1, :]) & (key < span_ref[1:2, :])


def attend_body(chunks, span_ref, q_ref, k_ref, v_ref, o_ref, lse_ref, acc_ref, top_ref):
    block = pl.program_id(1)
    q_pair = q_ref[...]
    zero = jnp.zeros_like(q_pair)
    queries = [jnp.where(head_lanes(q_pair.shape, h), q_pair, zero) for h in range(2)]
    acc_ref[...] = jnp.zeros_like(acc_ref)
    top_ref[...] = jnp.full_like(top_ref, 2 * big_negative)

    @pl.loop(chunks[block, 0], chunks[block, 1])
    def _(chunk):
        at = pl.multiple_of(chunk * BLOCK, BLOCK)
        keys = k_ref[pl.ds(at, BLOCK), :]
        values = v_ref[pl.ds(at, BLOCK), :]
        ok = inside(span_ref, at, (BLOCK, BLOCK))
        for h in range(2):
            scores = jnp.where(ok, dot_nt(keys, queries[h]), big_negative)
            old_top = top_ref[h : h + 1, :]
            top = jnp.maximum(old_top, jnp.max(scores, axis=0, keepdims=True))
            weights = jnp.exp(scores - top).astype(bf16)
            widened = jnp.where(head_lanes(values.shape, h), values, jnp.ones_like(values))
            acc_ref[h] = acc_ref[h] * jnp.exp(old_top - top) + dot_tn(widened, weights)
            top_ref[h : h + 1, :] = top

    sums = [acc_ref[0, HEAD_DIM : HEAD_DIM + 1, :], acc_ref[1, 0:1, :]]
    both = jnp.concatenate(
        [acc_ref[0, :HEAD_DIM, :] / sums[0], acc_ref[1, HEAD_DIM:, :] / sums[1]], axis=0
    )
    o_ref[...] = both.T.astype(bf16)
    for h in range(2):
        lse_ref[h : h + 1, :] = top_ref[h : h + 1, :] + jnp.log(sums[h])


def attend(chunks, span, q, k, v):
    own_rows, width = q.shape
    total = k.shape[0]
    pairs = width // PAIR
    return pl.pallas_call(
        attend_body,
        grid_spec=pltpu.PrefetchScalarGridSpec(
            num_scalar_prefetch=1,
            grid=(pairs, own_rows // BLOCK),
            in_specs=[
                pl.BlockSpec((8, BLOCK), lambda p, b, c: (0, b)),
                pl.BlockSpec((BLOCK, PAIR), lambda p, b, c: (b, p)),
                pl.BlockSpec((total, PAIR), lambda p, b, c: (0, p)),
                pl.BlockSpec((total, PAIR), lambda p, b, c: (0, p)),
            ],
            out_specs=[
                pl.BlockSpec((BLOCK, PAIR), lambda p, b, c: (b, p)),
                pl.BlockSpec((None, 8, BLOCK), lambda p, b, c: (p, 0, b)),
            ],
            scratch_shapes=[pltpu.VMEM((2, PAIR, BLOCK), f32), pltpu.VMEM((8, BLOCK), f32)],
        ),
        out_shape=[
            jax.ShapeDtypeStruct((own_rows, width), bf16),
            jax.ShapeDtypeStruct((pairs, 8, own_rows), f32),
        ],
        compiler_params=params(),
        name="attend",
    )(chunks, span, q, k, v)


def attend_back_body(
    ahead,
    chunks,
    span_ref,
    q_ref,
    k_ref,
    v_ref,
    o_ref,
    go_ref,
    lse_ref,
    cos_ref,
    sin_ref,
    gq_ref,
    gk_ref,
    gv_ref,
    accq_ref,
    acck_ref,
    accv_ref,
):
    block = pl.program_id(1)

    @pl.when(block == 0)
    def _():
        acck_ref[...] = jnp.zeros_like(acck_ref)
        accv_ref[...] = jnp.zeros_like(accv_ref)

    accq_ref[...] = jnp.zeros_like(accq_ref)
    q_pair = q_ref[...]
    go_pair = go_ref[...]
    zero = jnp.zeros_like(q_pair)
    queries = [jnp.where(head_lanes(q_pair.shape, h), q_pair, zero) for h in range(2)]
    grads = [jnp.where(head_lanes(q_pair.shape, h), go_pair, zero) for h in range(2)]
    products = (o_ref[...].astype(f32) * go_pair.astype(f32)).T
    inner = [
        jnp.sum(products[h * HEAD_DIM : (h + 1) * HEAD_DIM, :], axis=0, keepdims=True)
        for h in range(2)
    ]
    lse = [lse_ref[h : h + 1, :] for h in range(2)]

    @pl.loop(chunks[block, 0], chunks[block, 1])
    def _(chunk):
        at = pl.multiple_of(chunk * BLOCK, BLOCK)
        rows = pl.ds(at, BLOCK)
        keys = k_ref[rows, :]
        values = v_ref[rows, :]
        ok = inside(span_ref, at, (BLOCK, BLOCK))
        grad_k = acck_ref[rows, :]
        grad_v = accv_ref[rows, :]
        for h in range(2):
            scores = jnp.where(ok, dot_nt(keys, queries[h]), big_negative)
            probs = jnp.exp(scores - lse[h])
            grad_probs = dot_nt(values, grads[h])
            grad_v = grad_v + dot_nn(probs.astype(bf16), grads[h])
            grad_scores = (probs * (grad_probs - inner[h])).astype(bf16)
            grad_k = grad_k + dot_nn(grad_scores, queries[h])
            accq_ref[h] = accq_ref[h] + dot_tn(keys, grad_scores)
        acck_ref[rows, :] = grad_k
        accv_ref[rows, :] = grad_v

    both = jnp.concatenate([accq_ref[0, :HEAD_DIM, :], accq_ref[1, HEAD_DIM:, :]], axis=0)
    at = pl.multiple_of((block + ahead) * BLOCK, BLOCK)
    grad_q = both.T * (HEAD_DIM**-0.5)
    gq_ref[...] = turn(
        grad_q, cos_ref[pl.ds(at, BLOCK), :], -sin_ref[pl.ds(at, BLOCK), :]
    ).astype(bf16)

    @pl.when(block == pl.num_programs(1) - 1)
    def _():
        @pl.loop(0, gk_ref.shape[0] // BLOCK)
        def _(part):
            rows = pl.ds(pl.multiple_of(part * BLOCK, BLOCK), BLOCK)
            gk_ref[rows, :] = turn(acck_ref[rows, :], cos_ref[rows, :], -sin_ref[rows, :]).astype(
                bf16
            )
            gv_ref[rows, :] = accv_ref[rows, :].astype(bf16)


def attend_back(chunks, span, q, k, v, o, go, lse, cosine, sine):
    own_rows, width = q.shape
    total = k.shape[0]
    pairs = width // PAIR
    own_spec = pl.BlockSpec((BLOCK, PAIR), lambda p, b, c: (b, p))
    all_spec = pl.BlockSpec((total, PAIR), lambda p, b, c: (0, p))
    fixed = pl.BlockSpec((total, PAIR), lambda p, b, c: (0, 0), pipeline_mode=pl.Buffered(1))
    return pl.pallas_call(
        functools.partial(attend_back_body, MAX_LENGTH // BLOCK),
        grid_spec=pltpu.PrefetchScalarGridSpec(
            num_scalar_prefetch=1,
            grid=(pairs, own_rows // BLOCK),
            in_specs=[
                pl.BlockSpec((8, BLOCK), lambda p, b, c: (0, b)),
                own_spec,
                all_spec,
                all_spec,
                own_spec,
                own_spec,
                pl.BlockSpec((None, 8, BLOCK), lambda p, b, c: (p, 0, b)),
                fixed,
                fixed,
            ],
            out_specs=[own_spec, all_spec, all_spec],
            scratch_shapes=[
                pltpu.VMEM((2, PAIR, BLOCK), f32),
                pltpu.VMEM((total, PAIR), f32),
                pltpu.VMEM((total, PAIR), f32),
            ],
        ),
        out_shape=[
            jax.ShapeDtypeStruct((own_rows, width), bf16),
            jax.ShapeDtypeStruct((total, width), bf16),
            jax.ShapeDtypeStruct((total, width), bf16),
        ],
        compiler_params=params(),
        name="attend_back",
    )(chunks, span, q, k, v, o, go, lse, cosine, sine)


def middle_body(
    o_ref,
    x_ref,
    gy_ref,
    g_ref,
    wo_ref,
    wi_ref,
    wd_ref,
    y_ref,
    n_ref,
    m_ref,
    gu_ref,
    gh_ref,
    go_ref,
    dg_ref,
):
    hidden = wd_ref.shape[0]
    gain = g_ref[...]
    h2 = x_ref[...].astype(f32) + dot_nn(o_ref[...], wo_ref[...])
    normed, scale = normalized(h2)
    n2 = (normed * gain).astype(bf16)
    n_ref[...] = n2
    gate = dot_nn(n2, wi_ref[:, :hidden])
    linear = dot_nn(n2, wi_ref[:, hidden:])
    half_up = 0.5 + 0.5 * lax.erf(gate * math.sqrt(0.5))
    bell = jnp.exp(gate * gate * -0.5) * (1.0 / math.sqrt(2.0 * math.pi))
    activated = gate * half_up
    m = (activated * linear).astype(bf16)
    m_ref[...] = m
    y_ref[...] = (h2 + dot_nn(m, wd_ref[...])).astype(bf16)
    gy = gy_ref[...]
    gm = dot_nt(gy, wd_ref[...])
    ga = (gm * linear * (half_up + gate * bell)).astype(bf16)
    gb = (gm * activated).astype(bf16)
    gu_ref[:, :hidden] = ga
    gu_ref[:, hidden:] = gb
    gn = dot_nt(ga, wi_ref[:, :hidden]) + dot_nt(gb, wi_ref[:, hidden:])

    @pl.when(pl.program_id(0) == 0)
    def _():
        dg_ref[...] = jnp.zeros_like(dg_ref)

    product = gn * normed
    dg_ref[...] += jnp.broadcast_to(jnp.sum(product, axis=0, keepdims=True), dg_ref.shape)
    weighted = gn * gain
    gh2 = gy.astype(f32) + scale * (
        weighted
        - jnp.mean(weighted, axis=-1, keepdims=True)
        - normed * jnp.mean(weighted * normed, axis=-1, keepdims=True)
    )
    ghb = gh2.astype(bf16)
    gh_ref[...] = ghb
    go_ref[...] = dot_nt(ghb, wo_ref[...]).astype(bf16)


def middle(o, x, gy, gain, w_out, w_in, w_down):
    rows, width = x.shape
    hidden = w_down.shape[0]
    row = pl.BlockSpec((BLOCK, width), lambda i: (i, 0))
    whole = lambda a: pl.BlockSpec(a.shape, lambda i: (0, 0), pipeline_mode=pl.Buffered(1))
    wide = lambda n: pl.BlockSpec((BLOCK, n), lambda i: (i, 0))
    shape = lambda n: jax.ShapeDtypeStruct((rows, n), bf16)
    return pl.pallas_call(
        middle_body,
        grid=(rows // BLOCK,),
        in_specs=[row, row, row, whole(gain), whole(w_out), whole(w_in), whole(w_down)],
        out_specs=[
            row,
            row,
            wide(hidden),
            wide(2 * hidden),
            row,
            row,
            pl.BlockSpec((8, width), lambda i: (0, 0)),
        ],
        out_shape=[
            shape(width),
            shape(width),
            shape(hidden),
            shape(2 * hidden),
            shape(width),
            shape(width),
            jax.ShapeDtypeStruct((8, width), f32),
        ],
        compiler_params=params(),
        name="middle",
    )(o, x, gy, gain, w_out, w_in, w_down)


def split_store(product, core, group_count, keep_ref, send_ref):
    half = product.shape[0] // group_count // 2
    for owner in range(group_count):
        at = owner * 2 * half
        lower = product[at : at + half].astype(bf16)
        upper = product[at + half : at + 2 * half].astype(bf16)
        keep_ref[owner * half : (owner + 1) * half, :] = jnp.where(core == 0, lower, upper)
        send_ref[owner * half : (owner + 1) * half, :] = jnp.where(core == 0, upper, lower)


def weight_grad_body(group_count, core, left_ref, right_ref, keep_ref, send_ref):
    split_store(dot_tn(left_ref[...], right_ref[...]), core[0], group_count, keep_ref, send_ref)


def weight_grad(core, left, right, group_count, columns):
    rows, tall = left.shape
    wide = right.shape[1]
    result = pl.BlockSpec((tall // 2, columns), lambda i, c: (0, i))
    return pl.pallas_call(
        functools.partial(weight_grad_body, group_count),
        grid_spec=pltpu.PrefetchScalarGridSpec(
            num_scalar_prefetch=1,
            grid=(wide // columns,),
            in_specs=[
                pl.BlockSpec((rows, tall), lambda i, c: (0, 0), pipeline_mode=pl.Buffered(1)),
                pl.BlockSpec((rows, columns), lambda i, c: (0, i)),
            ],
            out_specs=[result, result],
        ),
        out_shape=[jax.ShapeDtypeStruct((tall // 2, wide), bf16)] * 2,
        compiler_params=params(),
        name="weight_grad",
    )(core, left, right)


def qkv_grad_body(
    ahead, own, group_count, info, n_ref, gq_ref, gk_ref, gv_ref, keep_ref, send_ref, acc_ref
):
    step = pl.program_id(0)
    width = n_ref.shape[1]

    @pl.when(step == 0)
    def _():
        acc_ref[...] = jnp.zeros_like(acc_ref)

    @pl.when((step >= info[0]) & (step < info[1]))
    def _():
        n1 = n_ref[...]
        acc_ref[:, width : 2 * width] += dot_tn(n1, gk_ref[...])
        acc_ref[:, 2 * width :] += dot_tn(n1, gv_ref[...])

        @pl.when((step >= ahead) & (step < ahead + own))
        def _():
            acc_ref[:, :width] += dot_tn(n1, gq_ref[...])

    @pl.when(step == pl.num_programs(0) - 1)
    def _():
        split_store(acc_ref, info[2], group_count, keep_ref, send_ref)


def qkv_grad(info, n1, gq, gk, gv, group_count):
    total, width = n1.shape
    ahead = MAX_LENGTH // BLOCK
    own = gq.shape[0] // BLOCK
    row = pl.BlockSpec((BLOCK, width), lambda i, s: (i, 0))
    own_row = pl.BlockSpec((BLOCK, width), lambda i, s: (jnp.clip(i - ahead, 0, own - 1), 0))
    result = pl.BlockSpec((width // 2, 3 * width), lambda i, s: (0, 0), pipeline_mode=pl.Buffered(1))
    return pl.pallas_call(
        functools.partial(qkv_grad_body, ahead, own, group_count),
        grid_spec=pltpu.PrefetchScalarGridSpec(
            num_scalar_prefetch=1,
            grid=(total // BLOCK,),
            in_specs=[row, own_row, row, row],
            out_specs=[result, result],
            scratch_shapes=[pltpu.VMEM((width, 3 * width), f32)],
        ),
        out_shape=[jax.ShapeDtypeStruct((width // 2, 3 * width), bf16)] * 2,
        compiler_params=params(),
        name="qkv_grad",
    )(info, n1, gq, gk, gv)


def input_grad_body(
    ahead, own, info, x_ref, gq_ref, gk_ref, gv_ref, w_ref, own_ref, before_ref, after_ref, dg_ref
):
    step = pl.program_id(0)
    width = x_ref.shape[1]
    is_own = (step >= ahead) & (step < ahead + own)
    needed = (step >= info[0]) & (step < info[1])

    @pl.when(step == 0)
    def _():
        dg_ref[...] = jnp.zeros_like(dg_ref)

    def count(gn):
        normed, _ = normalized(x_ref[...].astype(f32))
        dg_ref[...] += jnp.broadcast_to(
            jnp.sum(gn * normed, axis=0, keepdims=True), dg_ref.shape
        )

    def shared():
        return dot_nt(gk_ref[...], w_ref[:, width : 2 * width]) + dot_nt(
            gv_ref[...], w_ref[:, 2 * width :]
        )

    @pl.when(is_own)
    def _():
        gn = shared() + dot_nt(gq_ref[...], w_ref[:, :width])
        own_ref[...] = gn
        count(gn)

    for ref, here in ((before_ref, step < ahead), (after_ref, step >= ahead + own)):

        @pl.when(here & needed)
        def _():
            gn = shared()
            ref[...] = gn.astype(bf16)
            count(gn)

        @pl.when(here & jnp.logical_not(needed))
        def _():
            ref[...] = jnp.zeros_like(ref)


def gradient_rows(info, x, gq, gk, gv, w_qkv):
    total, width = x.shape
    ahead = MAX_LENGTH // BLOCK
    own = gq.shape[0] // BLOCK
    row = pl.BlockSpec((BLOCK, width), lambda i, s: (i, 0))
    own_row = pl.BlockSpec((BLOCK, width), lambda i, s: (jnp.clip(i - ahead, 0, own - 1), 0))
    return pl.pallas_call(
        functools.partial(input_grad_body, ahead, own),
        grid_spec=pltpu.PrefetchScalarGridSpec(
            num_scalar_prefetch=1,
            grid=(total // BLOCK,),
            in_specs=[
                row,
                own_row,
                row,
                row,
                pl.BlockSpec(w_qkv.shape, lambda i, s: (0, 0), pipeline_mode=pl.Buffered(1)),
            ],
            out_specs=[
                own_row,
                pl.BlockSpec((BLOCK, width), lambda i, s: (jnp.minimum(i, ahead - 1), 0)),
                pl.BlockSpec((BLOCK, width), lambda i, s: (jnp.maximum(i - ahead - own, 0), 0)),
                pl.BlockSpec((8, width), lambda i, s: (0, 0)),
            ],
        ),
        out_shape=[
            jax.ShapeDtypeStruct((own * BLOCK, width), f32),
            jax.ShapeDtypeStruct((MAX_LENGTH, width), bf16),
            jax.ShapeDtypeStruct((MAX_LENGTH, width), bf16),
            jax.ShapeDtypeStruct((8, width), f32),
        ],
        compiler_params=params(),
        name="gradient_rows",
    )(info, x, gq, gk, gv, w_qkv)


def finish_body(ahead, own, x_ref, gh_ref, gn_ref, before_ref, after_ref, g_ref, out_ref):
    step = pl.program_id(0)
    gn = gn_ref[...]
    gn = gn + jnp.where(step >= own - ahead, before_ref[...].astype(f32), 0.0)
    gn = gn + jnp.where(step < ahead, after_ref[...].astype(f32), 0.0)
    normed, scale = normalized(x_ref[...].astype(f32))
    weighted = gn * g_ref[...]
    out_ref[...] = (
        gh_ref[...].astype(f32)
        + scale
        * (
            weighted
            - jnp.mean(weighted, axis=-1, keepdims=True)
            - normed * jnp.mean(weighted * normed, axis=-1, keepdims=True)
        )
    ).astype(bf16)


def finish(x, gh, gn, before, after, gain):
    rows, width = x.shape
    ahead = MAX_LENGTH // BLOCK
    own = rows // BLOCK
    row = pl.BlockSpec((BLOCK, width), lambda i: (i, 0))
    return pl.pallas_call(
        functools.partial(finish_body, ahead, own),
        grid=(own,),
        in_specs=[
            row,
            row,
            row,
            pl.BlockSpec((BLOCK, width), lambda i: (jnp.maximum(i - own + ahead, 0), 0)),
            pl.BlockSpec((BLOCK, width), lambda i: (jnp.minimum(i, ahead - 1), 0)),
            pl.BlockSpec((1, width), lambda i: (0, 0)),
        ],
        out_specs=row,
        out_shape=jax.ShapeDtypeStruct((rows, width), bf16),
        compiler_params=params(),
        name="finish",
    )(x, gh, gn, before, after, gain)


def swap(values, axis, size, distance):
    return lax.ppermute(values, axis, [(i, i ^ distance) for i in range(size)])


def place_body(group_count, count, info, *refs):
    pieces = refs[:count]
    out_ref, sem = refs[count], refs[count + 1]
    half = out_ref.shape[0] // group_count // 2
    copies = []
    for side in range(2):
        for j in range(group_count):
            source = pieces[side * group_count + j]
            at = (info[0] ^ j) * 2 * half + (info[1] ^ side) * half
            copies.append(
                pltpu.make_async_copy(
                    source.at[pl.ds(0, half), :],
                    out_ref.at[pl.ds(pl.multiple_of(at, half), half), :],
                    sem.at[len(copies)],
                )
            )
    for copy in copies:
        copy.start()
    for copy in copies:
        copy.wait()


def place(info, pieces, group_count, rows):
    any_spec = pl.BlockSpec(memory_space=pl.ANY)
    return pl.pallas_call(
        functools.partial(place_body, group_count, len(pieces)),
        in_specs=[pl.BlockSpec(memory_space=pltpu.SMEM)] + [any_spec] * len(pieces),
        out_specs=any_spec,
        out_shape=jax.ShapeDtypeStruct((rows, pieces[0].shape[1]), pieces[0].dtype),
        scratch_shapes=[pltpu.SemaphoreType.DMA((len(pieces),))],
        name="place",
    )(info, *pieces)


def fetch(half_shard, sizes):
    mine = [half_shard]
    for j in range(1, sizes["group"]):
        mine.append(swap(half_shard, "group", sizes["group"], j))
    return mine + [swap(piece, "replica", sizes["replica"], 1) for piece in mine]


def total(keep, send, group, sizes):
    groups, replicas = sizes["group"], sizes["replica"]
    got = swap(send, "replica", replicas, 1)
    both = (keep.astype(f32) + got.astype(f32)).astype(bf16)
    blocks = both.reshape(groups, both.shape[0] // groups, both.shape[1])
    pick = lambda j: lax.dynamic_index_in_dim(blocks, group ^ j, 0, keepdims=False)
    part = pick(0).astype(f32)
    for j in range(1, groups):
        part = part + swap(pick(j), "group", groups, j).astype(f32)
    distance = 2
    while distance < replicas:
        part = part.astype(bf16)
        part = part.astype(f32) + swap(part, "replica", replicas, distance).astype(f32)
        distance *= 2
    part = part.astype(bf16)
    other = swap(part, "replica", replicas, 1)
    first = lax.axis_index("replica") % 2 == 0
    return jnp.concatenate(
        [jnp.where(first, part, other), jnp.where(first, other, part)], axis=0
    ).astype(f32)


def total_small(values, sizes):
    for axis in ("replica", "group"):
        distance = 1
        while distance < sizes[axis]:
            values = values + swap(values, axis, sizes[axis], distance)
            distance *= 2
    return values


def plan(lengths, base, total_rows, own_rows):
    ends = jnp.cumsum(lengths)
    starts = ends - lengths
    at = base + jnp.arange(total_rows, dtype=jnp.int32)
    in_seq = (at[:, None] >= starts[None, :]) & (at[:, None] < ends[None, :])
    low = jnp.sum(jnp.where(in_seq, starts[None, :], 0), axis=1)
    high = jnp.sum(jnp.where(in_seq, ends[None, :], 0), axis=1)
    return low, high, at - low


def on_device(
    sizes,
    tokens,
    cotangent,
    lengths,
    dealing,
    offsets,
    attn_gain,
    qkv_weight,
    out_weight,
    mlp_gain,
    in_weight,
    down_weight,
):
    own_rows, width = tokens.shape[1:]
    groups, replicas = sizes["group"], sizes["replica"]
    group = lax.axis_index("group")
    replica = lax.axis_index("replica")
    core = replica % 2
    x = tokens[0]
    gy = cotangent[0]

    up = [(i, i + 1) for i in range(replicas - 1)]
    down = [(i + 1, i) for i in range(replicas - 1)]
    rows = jnp.concatenate(
        [
            lax.ppermute(x[own_rows - MAX_LENGTH :], "replica", up),
            x,
            lax.ppermute(x[:MAX_LENGTH], "replica", down),
        ],
        axis=0,
    )
    all_rows = own_rows + 2 * MAX_LENGTH

    gains = jnp.zeros((8, qkv_weight.shape[1]), bf16)
    gains = gains.at[0, : attn_gain.shape[0]].set(attn_gain.astype(bf16))
    gains = gains.at[1, : mlp_gain.shape[0]].set(mlp_gain.astype(bf16))

    def half_of(weight):
        half = weight.shape[0] // 2
        return lax.dynamic_slice_in_dim(weight, core * half, half, 0).astype(bf16)

    where = jnp.stack([group, core]).astype(jnp.int32)
    pieces = fetch(jnp.concatenate([half_of(qkv_weight), gains], axis=0), sizes)
    w_qkv = place(where, pieces, groups, groups * qkv_weight.shape[0])
    shard = attn_gain.shape[0]
    near = jnp.stack([piece[-8:-6, :shard].astype(f32) for piece in pieces[:groups]])
    order = jnp.arange(groups)[:, None] ^ group == jnp.arange(groups)[None, :]
    both_gains = jnp.sum(jnp.where(order[:, :, None, None], near[None], 0.0), axis=1)
    gain_one = both_gains[:, 0].reshape(1, width)
    gain_two = both_gains[:, 1].reshape(1, width)
    w_out = place(where, fetch(half_of(out_weight), sizes), groups, groups * out_weight.shape[0])
    w_in = place(where, fetch(half_of(in_weight), sizes), groups, groups * in_weight.shape[0])
    w_down = place(where, fetch(half_of(down_weight), sizes), groups, groups * down_weight.shape[0])

    base = replica * own_rows - MAX_LENGTH
    low, high, positions = plan(lengths[0], base, all_rows, own_rows)
    own_low = low[MAX_LENGTH : MAX_LENGTH + own_rows] - base
    own_high = high[MAX_LENGTH : MAX_LENGTH + own_rows] - base
    span = jnp.concatenate(
        [own_low[None], own_high[None], jnp.zeros((6, own_rows), jnp.int32)], axis=0
    )
    chunks = jnp.stack(
        [
            own_low.reshape(-1, BLOCK)[:, 0] // BLOCK,
            (own_high.reshape(-1, BLOCK)[:, -1] + BLOCK - 1) // BLOCK,
        ],
        axis=1,
    ).astype(jnp.int32)
    info = jnp.stack([chunks[0, 0], chunks[-1, 1], core]).astype(jnp.int32)

    half_dim = HEAD_DIM // 2
    frequency = jnp.exp(
        -(jnp.arange(half_dim, dtype=f32) * (2.0 / HEAD_DIM)) * math.log(rope_base)
    )
    angles = positions.astype(f32)[:, None] * jnp.tile(frequency, PAIR // half_dim)[None, :]
    sign = jnp.where(jnp.arange(PAIR) % HEAD_DIM < half_dim, -1.0, 1.0).astype(f32)
    cosine = jnp.cos(angles)
    sine = jnp.sin(angles) * sign[None, :]

    n1, q, k, v = project(info, rows, gain_one, w_qkv, cosine, sine, own_rows)
    attended, lse = attend(chunks, span, q, k, v)
    y, n2, m, gu, gh, go, dg_two = middle(attended, x, gy, gain_two, w_out, w_in, w_down)

    core_info = core.reshape(1).astype(jnp.int32)
    down_grad = total(*weight_grad(core_info, m, gy, groups, width // 2), group, sizes)
    in_grad = total(*weight_grad(core_info, n2, gu, groups, width), group, sizes)
    out_grad = total(*weight_grad(core_info, attended, gh, groups, width // 2), group, sizes)

    gq, gk, gv = attend_back(chunks, span, q, k, v, attended, go, lse, cosine, sine)
    qkv_parts = qkv_grad(info, n1, gq, gk, gv, groups)
    gn, before, after, dg_one = gradient_rows(info, rows, gq, gk, gv, w_qkv)
    qkv_sum = total(*qkv_parts, group, sizes)
    before = lax.ppermute(before, "replica", down)
    after = lax.ppermute(after, "replica", up)
    gx = finish(x, gh, gn, before, after, gain_one)

    dg = total_small(jnp.stack([dg_one[0], dg_two[0]]), sizes)
    dg = lax.dynamic_slice_in_dim(dg, group * shard, shard, 1)
    return y[None], gx[None], dg[0], qkv_sum, out_grad, dg[1], in_grad, down_grad


def solution(mesh):
    sizes = dict(mesh.shape)
    return jax.shard_map(
        functools.partial(on_device, sizes),
        mesh=mesh,
        in_specs=(
            P("group", "replica", None),
            P("group", "replica", None),
            P("group", None),
            P("group", None),
            P("group", None, None),
            P("group"),
            P("group", None),
            P("group", None),
            P("group"),
            P("group", None),
            P("group", None),
        ),
        out_specs=(
            P("group", "replica", None),
            P("group", "replica", None),
            P("group"),
            P("group", None),
            P("group", None),
            P("group"),
            P("group", None),
            P("group", None),
        ),
        check_vma=False,
    )
```
